32 devices in a mesh: front: 4 (over y, core), row: 8 (over z, x).
Axes of the slice: x: 2, y: 2, z: 4, core: 2. Of those that a mesh axis runs over, the one named last changes fastest.
Arguments:
- rhs_diag: float32 [4, 32, 2048], P('front', None, 'row'), may hold values from -6 to 6
- rhs_off: float32 [4, 32, 12288], P('front', None, 'row'), may hold values from -6 to 6
- diag_factor: float32 [4, 2048, 2048], P('front', 'row'), may hold values from -0.125 to 0.125
- off_factor: float32 [4, 12288, 2048], P('front', 'row'), may hold values from -0.125 to 0.125
- diag_inverse: float32 [4, 4, 512, 512], P('front')
- pattern: int32 [4, 4, 96], P('front', None, 'row'), may hold values 0 or 1
- upd_vals: float32 [32, 4, 8, 4, 8, 128], P(None, 'front', 'row'), may hold values from -4 to 4
- upd_rows: int32 [4, 8, 4, 8, 128], P('front', 'row'), may hold values from 0 to 1791
Outputs:
- solved: float32 [4, 32, 2048], P('front', None, 'row')
- remainder: float32 [4, 32, 12288], P('front', None, 'row')
The draws below stay inside these ranges and needn't reach their ends.
Inputs may be any that keep to these rules, and one draw needn't show every extreme that they name: `upd_rows`: relative rows of the receiving row block: below 256 a window row, else a row below the window; several entries may name one row.
All inputs are finite; a program needn't handle non-finite values. No bound on the sum of `pattern` on one device may be relied on, other than what follows from the above.
Results may differ from the reference program's by a relative error of at most 0.0001.
Values sent between devices are 32-bit elements; how exact they have to be, the bound alone decides.
A program may use at most 128 MiB of HBM per device.

```python
import jax
import jax.numpy as jnp
from jax import lax

W = 512
P_SIZE = 4
NRHS = 32
BR = 128
OFF_DEV = 1536
SLOT = 128
K = 2048
RD = 256
OFF = 12288
OFFB = 96
FRONTS = 4
ROWG = 8


def draw_diag_inverse(key, part):
    first_key, second_key = jax.random.split(key)
    shape = (FRONTS, P_SIZE, W, W)
    row_index = lax.broadcasted_iota(jnp.int32, shape, 2)
    col_index = lax.broadcasted_iota(jnp.int32, shape, 3)
    below = jax.random.normal(first_key, shape, jnp.float32)
    diagonal_vals = jax.random.uniform(second_key, shape, jnp.float32, 1.0, 2.0)
    scaled = below * (1.0 / W ** 0.5)
    return jnp.where(row_index > col_index, scaled, jnp.where(row_index == col_index, diagonal_vals, 0.0))


def touch_ends(values, stream_key, least, high):
    shape = values.shape
    place = [jax.random.randint(jax.random.fold_in(stream_key, axis), (), 0, shape[axis]) for axis in range(len(shape))]
    values = values.at[tuple(place)].set(least)
    longest = shape.index(max(shape))
    place[longest] = (place[longest] + 1) % shape[longest]
    return values.at[tuple(place)].set(high)


def levels(key, dims, cuts, low, top_value):
    factor_of = 1.0
    for dim, shards_of in cuts:
        heights = jax.random.uniform(jax.random.fold_in(jax.random.fold_in(key, 6), dim), (shards_of,), jnp.float32, low / len(cuts), top_value / len(cuts))
        factor_of = factor_of * jnp.repeat(jnp.exp(heights), dims[dim] // shards_of).reshape((-1,) + (1,) * (len(dims) - 1 - dim))
    return factor_of


def normal_values(rng, extent, width, limit, cuts=(), kind=jnp.bfloat16):
    level = levels(rng, extent, cuts, -0.22, 0.18) if cuts else 1.0
    drawn = jax.random.normal(rng, extent, jnp.float32) * width * level
    return jnp.minimum(jnp.maximum(drawn, -limit), limit).astype(kind)


def setup_inputs(seed: int = 0) -> dict:
    arg_keys = jax.random.split(jax.random.key(seed), 9)
    return {
        "rhs_diag": normal_values(arg_keys[0], (FRONTS, NRHS, K), 1.0, 6.0, ((0, 4), (2, 8)), jnp.float32),
        "rhs_off": normal_values(arg_keys[1], (FRONTS, NRHS, OFF), 1.0, 6.0, ((0, 4), (2, 8)), jnp.float32),
        "diag_factor": normal_values(arg_keys[2], (FRONTS, K, K), K ** -0.5, 0.125, ((0, 4), (1, 8)), jnp.float32),
        "off_factor": normal_values(arg_keys[3], (FRONTS, OFF, K), K ** -0.5, 0.125, ((0, 4), (1, 8)), jnp.float32),
        "diag_inverse": draw_diag_inverse(jax.random.fold_in(arg_keys[8], 71), 0),
        "pattern": touch_ends((jax.random.randint(arg_keys[5], (FRONTS, P_SIZE, OFFB), 0, 4) < 3).astype(jnp.int32), jax.random.fold_in(arg_keys[5], 1), 0, 1),
        "upd_vals": normal_values(arg_keys[6], (NRHS, FRONTS, ROWG, FRONTS, ROWG, SLOT), 0.3, 4.0, ((1, 4), (2, 8)), jnp.float32),
        "upd_rows": touch_ends(jax.random.randint(arg_keys[7], (FRONTS, ROWG, FRONTS, ROWG, SLOT), 0, RD + OFF_DEV), jax.random.fold_in(arg_keys[7], 1), 0, (RD + OFF_DEV) - 1).astype(jnp.int32),
    }


def reference(rhs_diag, rhs_off, diag_factor, off_factor, diag_inverse, pattern, upd_vals, upd_rows):
    rows_all = K + OFF
    dst_front = lax.broadcasted_iota(jnp.int32, upd_rows.shape, 0)
    dst_group = lax.broadcasted_iota(jnp.int32, upd_rows.shape, 1)
    global_row = jnp.where(upd_rows < RD, dst_group * RD + upd_rows, K + dst_group * OFF_DEV + upd_rows - RD)
    flat_target = (dst_front * rows_all + global_row).reshape(-1).astype(jnp.int32)
    values = jnp.transpose(upd_vals, (0, 3, 4, 1, 2, 5)).reshape(NRHS, -1)
    whole = jnp.concatenate([rhs_diag, rhs_off], axis=2)
    flat_rhs = jnp.transpose(whole, (1, 0, 2)).reshape(NRHS, -1)
    flat_rhs = flat_rhs.at[:, flat_target].add(values)
    whole = jnp.transpose(flat_rhs.reshape(NRHS, FRONTS, rows_all), (1, 0, 2))
    upper = whole[:, :, :K]
    lower = whole[:, :, K:]
    highest = lax.Precision.HIGHEST
    pieces = []
    for panel in range(P_SIZE):
        panel_rhs = upper[:, :, panel * W:(panel + 1) * W]
        piece = jnp.einsum("fnb,fab->fna", panel_rhs, diag_inverse[:, panel], precision=highest)
        pieces.append(piece)
        upper = upper - jnp.einsum("fna,fca->fnc", piece, diag_factor[:, :, panel * W:(panel + 1) * W], precision=highest)
        mask_rows = jnp.repeat(pattern[:, panel, :].astype(jnp.float32), BR, axis=1)
        term = jnp.einsum("fna,fca->fnc", piece, off_factor[:, :, panel * W:(panel + 1) * W], precision=highest)
        lower = lower - term * mask_rows[:, None, :]
    return jnp.concatenate(pieces, axis=2), lower
```

```python
import functools

import jax
import jax.numpy as jnp
from jax import lax
from jax.experimental import pallas as pl
from jax.experimental.pallas import tpu as pltpu
from jax.sharding import PartitionSpec as P

W = 512
BR = 128
MESH = pl.DeviceIdType.MESH
PART = 256
NT = (((1,), (1,)), ((), ()))


def split(x):
    hi = x.astype(jnp.bfloat16)
    lo = (x - hi.astype(jnp.float32)).astype(jnp.bfloat16)
    return hi, lo


def dot_nt(a, b):
    return lax.dot_general(a, b, NT, preferred_element_type=jnp.float32)


def dot3(a2, b_hi, b_lo):
    n = a2.shape[0] // 2
    top = dot_nt(a2, b_hi)
    return top[:n] + top[n:] + dot_nt(a2[:n], b_lo)


def reach(planes, plane):
    orders = [sorted(range(planes), key=lambda q, z=z: (abs(q - z), q)) for z in range(planes)]
    out = []
    for i in range(planes):
        q = jnp.int32(orders[0][i])
        for z in range(1, planes):
            q = jnp.where(plane == z, jnp.int32(orders[z][i]), q)
        out.append(q)
    return out


def kernel(nf, nr, rd_hbm, ro_hbm, diag_hbm, off_hbm, inv_hbm, pat_hbm, vals_hbm, rows_hbm,
           solved_ref, rem_ref,
           diag_f, off_f, inv_f, diag_h, diag_l, off_h, off_l, inv_h, inv_l, step_h, step_l,
           recv, vs, hot, rows_v, code_ref, acc, upper, rhsbuf, rd_v, ro_v, pat_ref,
           load_sem, own_sem, a2a_send, a2a_recv, pan_send, pan_recv):
    f = lax.axis_index("front")
    r = lax.axis_index("row")
    devices = nf * nr
    nrhs, rd = upper.shape
    od = off_f.shape[0]
    panels = inv_f.shape[0]
    per = W // rd
    slot = recv.shape[3]
    members = nf * per
    plane = r // per
    place = lax.rem(r, per)
    me = f * nr + r

    barrier = pltpu.get_barrier_semaphore()

    def greet(d, c):
        pf = lax.rem(f + d // nr, nf)
        pr = lax.rem(r + lax.rem(d, nr), nr)
        pl.semaphore_signal(barrier, inc=1, device_id=(pf, pr), device_id_type=MESH)
        return c

    lax.fori_loop(1, devices, greet, 0)

    load_rows = pltpu.make_async_copy(rows_hbm, rows_v, load_sem.at[0])
    load_inv = pltpu.make_async_copy(inv_hbm.at[0], inv_f, load_sem.at[1])
    load_diag = pltpu.make_async_copy(diag_hbm.at[0], diag_f, load_sem.at[2])
    load_off = pltpu.make_async_copy(off_hbm.at[0], off_f, load_sem.at[3])
    load_rd = pltpu.make_async_copy(rd_hbm.at[0], rd_v, load_sem.at[4])
    load_ro = pltpu.make_async_copy(ro_hbm.at[0], ro_v, load_sem.at[5])
    load_pat = pltpu.make_async_copy(pat_hbm.at[0], pat_ref, load_sem.at[6])
    own = pltpu.make_async_copy(vals_hbm.at[:, f, r, :], recv.at[f, r], own_sem)
    for load in (load_rows, load_inv, load_diag, load_off, load_rd, load_ro, load_pat, own):
        load.start()

    def exchange(pf, pr, source):
        return pltpu.make_async_remote_copy(
            src_ref=vals_hbm.at[:, pf, pr, :],
            dst_ref=recv.at[source // nr, lax.rem(source, nr)],
            send_sem=a2a_send.at[pf * nr + pr],
            recv_sem=a2a_recv.at[source],
            device_id=(pf, pr),
            device_id_type=MESH,
        )

    pl.semaphore_wait(barrier, devices - 1)

    def target(t):
        i = lax.rem(t, members)
        pf = lax.rem(f + i // per, nf)
        pr = (t // members) * per + lax.rem(place + i, per)
        return pf, pr

    def send(t, c):
        pf, pr = target(t)

        @pl.when(pf * nr + pr != me)
        def _():
            exchange(pf, pr, me).start()

        return c

    lax.fori_loop(0, devices, send, 0)

    def source_of(s):
        i = lax.rem(s, members)
        return i // per, (s // members) * per + lax.rem(i, per)

    load_rows.wait()

    def mark(s, c):
        sf, sr = source_of(s)
        code = rows_v[pl.ds(sf * nr + sr, 1), :] + (PART - rd)
        code_ref[pl.ds(s, 1), :] = code
        ids = lax.broadcasted_iota(jnp.int32, (PART, slot), 0)
        at = pl.ds(pl.multiple_of(s * slot, slot), slot)
        hot[:, at] = jnp.where((code & (PART - 1)) == ids, 1.0, 0.0).astype(jnp.bfloat16)
        return c

    lax.fori_loop(0, devices, mark, 0)

    load_inv.wait()
    for p in range(panels):
        def split_inv(i, c, p=p):
            at = pl.ds(pl.multiple_of(i * 64, 64), 64)
            hi, lo = split(inv_f[p, at, :])
            inv_h[p, at, :] = hi
            inv_l[p, at, :] = lo
            return c

        lax.fori_loop(0, W // 64, split_inv, 0)
    load_diag.wait()

    def split_diag(i, c):
        at = pl.ds(pl.multiple_of(i * 16, 16), 16)
        hi, lo = split(diag_f[at, :])
        diag_h[at, :] = hi
        diag_l[at, :] = lo
        return c

    lax.fori_loop(0, rd // 16, split_diag, 0)

    for p in range(panels - 1):
        @pl.when(plane > p)
        def _(p=p):
            for n in range(2):
                columns = pl.ds(n * (W // 2), W // 2)
                left_h = diag_h[:, pl.ds(p * W, W)]
                left_l = diag_l[:, pl.ds(p * W, W)]
                right_h = inv_h[p, :, columns]
                product = (jnp.dot(left_h, right_h, preferred_element_type=jnp.float32)
                           + jnp.dot(left_l, right_h, preferred_element_type=jnp.float32)
                           + jnp.dot(left_h, inv_l[p, :, columns], preferred_element_type=jnp.float32))
                hi, lo = split(product)
                step_h[p, :, columns] = hi
                step_l[p, :, columns] = lo

    load_off.wait()

    def split_off(i, c):
        at = pl.ds(pl.multiple_of(i * 16, 16), 16)
        hi, lo = split(off_f[at, :])
        off_h[at, :] = hi
        off_l[at, :] = lo
        return c

    lax.fori_loop(0, od // 16, split_off, 0)

    group = 4
    span = group * slot
    per_plane = members // group
    chunk = 2 * BR
    chunks = od // chunk
    lower_parts = list(range(1, chunks + 1))

    def columns_of(g):
        return pl.ds(pl.multiple_of(g * span, span), span)

    def picked(g, parts):
        block = code_ref[pl.ds(pl.multiple_of(g * group, group), group), :]
        part = jnp.concatenate([block[u:u + 1, :] for u in range(group)], axis=1) >> 8
        values = vs[:, columns_of(g)]
        rows = []
        for h in parts:
            mask = jnp.where(jnp.broadcast_to(part, (16, span)) == h, 1.0, 0.0).astype(jnp.bfloat16)
            rows.append(values * jnp.concatenate([mask] * (2 * nrhs // 16), axis=0))
        return jnp.concatenate(rows, axis=0)

    def take(g):
        for u in range(group):
            s = g * group + u
            sf, sr = source_of(s)

            @pl.when(sf * nr + sr != me)
            def _(sf=sf, sr=sr):
                exchange(sf, sr, sf * nr + sr).wait_recv()

            hi, lo = split(recv[sf, sr])
            at = pl.ds(pl.multiple_of(s * slot, slot), slot)
            vs[pl.ds(0, nrhs), at] = hi
            vs[pl.ds(nrhs, nrhs), at] = lo

    upper_rows = pl.ds(0, 2 * nrhs)
    lower_rows = pl.ds(2 * nrhs, 2 * nrhs * chunks)

    def add_all(g):
        acc[...] += dot_nt(picked(g, [0] + lower_parts), hot[:, columns_of(g)])

    def add_upper(g):
        acc[upper_rows, :] += dot_nt(picked(g, [0]), hot[:, columns_of(g)])

    def add_lower(g):
        acc[lower_rows, :] += dot_nt(picked(g, lower_parts), hot[:, columns_of(g)])

    def reduced(h):
        at = 2 * h * nrhs
        return acc[at:at + nrhs, :] + acc[at + nrhs:at + 2 * nrhs, :]

    acc[...] = jnp.zeros_like(acc)
    load_rd.wait()
    load_ro.wait()
    load_pat.wait()
    own.wait()
    order = reach(panels, plane)
    for q in order[:-1]:
        def near(i, c, q=q):
            g = q * per_plane + i
            take(g)
            add_all(g)
            return c

        lax.fori_loop(0, per_plane, near, 0)

    def far(i, c):
        g = order[-1] * per_plane + i
        take(g)
        add_upper(g)
        return c

    lax.fori_loop(0, per_plane, far, 0)
    upper[...] = rd_v[...] + reduced(0)[:, PART - rd:]

    def scatter_lower():
        def step(i, c):
            add_lower(order[-1] * per_plane + i)
            return c

        lax.fori_loop(0, per_plane, step, 0)
        for h in range(chunks):
            at = pl.ds(h * chunk, chunk)
            rem_ref[0, :, at] = ro_v[:, at] + reduced(h + 1)

    def off_update(p, piece2):
        def step(i, c):
            at = pl.ds(pl.multiple_of(i * chunk, chunk), chunk)
            columns = pl.ds(p * W, W)
            term = dot3(piece2, off_h[at, columns], off_l[at, columns])
            scaled = jnp.concatenate(
                [term[:, b * BR:(b + 1) * BR] * pat_ref[p, 2 * i + b].astype(jnp.float32) for b in range(2)], axis=1)
            rem_ref[0, :, at] -= scaled
            return c

        lax.fori_loop(0, chunks, step, 0)

    def share(to, j):
        return pltpu.make_async_remote_copy(
            src_ref=rhsbuf.at[j],
            dst_ref=rhsbuf.at[j],
            send_sem=pan_send.at[to],
            recv_sem=pan_recv.at[j],
            device_id=(f, to),
            device_id_type=MESH,
        )

    def finish(p, b2):
        piece = dot3(b2, inv_h[p], inv_l[p])
        for i in range(per):
            @pl.when(r == p * per + i)
            def _(i=i):
                solved_ref[0] = piece[:, i * rd:(i + 1) * rd]
        off_update(p, jnp.concatenate(split(piece), axis=0))

    b2 = None
    for p in range(panels):
        @pl.when(plane == p)
        def _(p=p):
            rhsbuf[r] = upper[...]
            if p < panels - 1:
                targets = [(p + 1) * per + lax.rem(place + i, per) for i in range(per)]
                targets += [p * per + lax.rem(place + i, per) for i in range(1, per)]
                targets += [q * per + lax.rem(place + i, per)
                            for q in [*range(p + 2, panels), *range(p - 1, -1, -1)] for i in range(per)]
            else:
                targets = [q * per + i for q in range(panels - 1) for i in range(per)]
                targets += [p * per + lax.rem(place + i, per) for i in range(1, per)]
            for to in targets:
                share(to, r).start()

        if p == 0:
            scatter_lower()
        else:
            finish(p - 1, b2)

        for j in range(p * per, (p + 1) * per):
            @pl.when(r != j)
            def _(j=j):
                share(j, j).wait_recv()

        b = jnp.concatenate([rhsbuf[j] for j in range(p * per, (p + 1) * per)], axis=1)
        b2 = jnp.concatenate(split(b), axis=0)
        if p < panels - 1:
            @pl.when(plane > p)
            def _(b2=b2, p=p):
                upper[...] -= dot3(b2, step_h[p], step_l[p])

    finish(panels - 1, b2)

    def sent(t, c):
        pf, pr = target(t)

        @pl.when(pf * nr + pr != me)
        def _():
            exchange(pf, pr, me).wait_send()

        return c

    lax.fori_loop(0, devices, sent, 0)

    def shared(d, c):
        share(lax.rem(r + d, nr), r).wait_send()
        return c

    lax.fori_loop(1, nr, shared, 0)


def hand_out(solved_in, rem_in, solved_out, rem_out):
    solved_out[...] = solved_in[...]
    rem_out[...] = rem_in[...]


def local(nf, nr, rhs_diag, rhs_off, diag_factor, off_factor, diag_inverse, pattern, upd_vals, upd_rows):
    nrhs = upd_vals.shape[0]
    slot = upd_vals.shape[5]
    rd = diag_factor.shape[1]
    od = off_factor.shape[1]
    k = diag_factor.shape[2]
    panels = diag_inverse.shape[1]
    devices = nf * nr
    parts = od // PART + 1
    vals = upd_vals.reshape(upd_vals.shape[0], nf, nr, slot)
    rows = upd_rows.reshape(devices, slot)
    vmem = pl.BlockSpec(memory_space=pltpu.VMEM)
    anywhere = pl.BlockSpec(memory_space=pl.ANY)
    f32, bf16 = jnp.float32, jnp.bfloat16
    outs = (
        jax.ShapeDtypeStruct((1, nrhs, rd), f32),
        jax.ShapeDtypeStruct((1, nrhs, od), f32),
    )
    results = pl.pallas_call(
        functools.partial(kernel, nf, nr),
        out_shape=outs,
        in_specs=[anywhere] * 8,
        out_specs=(vmem, vmem),
        scratch_shapes=[
            pltpu.VMEM((rd, k), f32),
            pltpu.VMEM((od, k), f32),
            pltpu.VMEM((panels, W, W), f32),
            pltpu.VMEM((rd, k), bf16),
            pltpu.VMEM((rd, k), bf16),
            pltpu.VMEM((od, k), bf16),
            pltpu.VMEM((od, k), bf16),
            pltpu.VMEM((panels, W, W), bf16),
            pltpu.VMEM((panels, W, W), bf16),
            pltpu.VMEM((panels - 1, rd, W), bf16),
            pltpu.VMEM((panels - 1, rd, W), bf16),
            pltpu.VMEM((nf, nr, nrhs, slot), f32),
            pltpu.VMEM((2 * nrhs, devices * slot), bf16),
            pltpu.VMEM((PART, devices * slot), bf16),
            pltpu.VMEM((devices, slot), jnp.int32),
            pltpu.VMEM((devices, slot), jnp.int32),
            pltpu.VMEM((2 * nrhs * parts, PART), f32),
            pltpu.VMEM((nrhs, rd), f32),
            pltpu.VMEM((nr, nrhs, rd), f32),
            pltpu.VMEM((nrhs, rd), f32),
            pltpu.VMEM((nrhs, od), f32),
            pltpu.SMEM(pattern.shape[1:], jnp.int32),
            pltpu.SemaphoreType.DMA((7,)),
            pltpu.SemaphoreType.DMA,
            pltpu.SemaphoreType.DMA((devices,)),
            pltpu.SemaphoreType.DMA((devices,)),
            pltpu.SemaphoreType.DMA((nr,)),
            pltpu.SemaphoreType.DMA((nr,)),
        ],
        compiler_params=pltpu.CompilerParams(
            collective_id=0, has_side_effects=True, vmem_limit_bytes=58 * 1024 * 1024),
    )(rhs_diag, rhs_off, diag_factor, off_factor, diag_inverse, pattern, vals, rows)
    return pl.pallas_call(hand_out, out_shape=outs, in_specs=[vmem, vmem], out_specs=(vmem, vmem))(*results)


def solution(mesh):
    in_specs = (
        P("front", None, "row"),
        P("front", None, "row"),
        P("front", "row", None),
        P("front", "row", None),
        P("front", None, None, None),
        P("front", None, "row"),
        P(None, "front", "row", None, None, None),
        P("front", "row", None, None, None),
    )
    out_specs = (P("front", None, "row"), P("front", None, "row"))
    body = functools.partial(local, mesh.shape["front"], mesh.shape["row"])
    return jax.shard_map(body, mesh=mesh, in_specs=in_specs, out_specs=out_specs, check_vma=False)
```

```python
import functools

import jax
import jax.numpy as jnp
from jax import lax
from jax.experimental import pallas as pl
from jax.experimental.pallas import tpu as pltpu
from jax.sharding import PartitionSpec as P

W = 512
BR = 128
MESH = pl.DeviceIdType.MESH
PART = 256
CUTS = 1
NT = (((1,), (1,)), ((), ()))


def split(x):
    hi = x.astype(jnp.bfloat16)
    lo = (x - hi.astype(jnp.float32)).astype(jnp.bfloat16)
    return hi, lo


def dot_nt(a, b):
    return lax.dot_general(a, b, NT, preferred_element_type=jnp.float32)


def dot3(a2, b_hi, b_lo):
    n = a2.shape[0] // 2
    top = dot_nt(a2, b_hi)
    return top[:n] + top[n:] + dot_nt(a2[:n], b_lo)


def reach(planes, plane):
    orders = [sorted(range(planes), key=lambda q, z=z: (abs(q - z), q)) for z in range(planes)]
    out = []
    for i in range(planes):
        q = jnp.int32(orders[0][i])
        for z in range(1, planes):
            q = jnp.where(plane == z, jnp.int32(orders[z][i]), q)
        out.append(q)
    return out


def kernel(nf, nr, rd_hbm, ro_hbm, diag_hbm, off_hbm, inv_hbm, pat_hbm, vals_hbm, rows_hbm,
           solved_ref, rem_ref,
           diag_f, off_f, inv_f, diag_h, diag_l, off_h, off_l, inv_h, inv_l, step_h, step_l,
           recv, vs, hot, rows_v, code_ref, acc, upper, rhsbuf, rd_v, ro_v, pat_ref,
           load_sem, own_sem, a2a_send, a2a_recv, pan_send, pan_recv):
    f = lax.axis_index("front")
    r = lax.axis_index("row")
    devices = nf * nr
    nrhs, rd = upper.shape
    od = off_f.shape[0]
    panels = inv_f.shape[0]
    per = W // rd
    slot = recv.shape[3]
    members = nf * per
    plane = r // per
    place = lax.rem(r, per)
    me = f * nr + r

    barrier = pltpu.get_barrier_semaphore()

    def greet(d, c):
        pf = lax.rem(f + d // nr, nf)
        pr = lax.rem(r + lax.rem(d, nr), nr)
        pl.semaphore_signal(barrier, inc=1, device_id=(pf, pr), device_id_type=MESH)
        return c

    lax.fori_loop(1, devices, greet, 0)

    load_rows = pltpu.make_async_copy(rows_hbm, rows_v, load_sem.at[0])
    load_inv = pltpu.make_async_copy(inv_hbm.at[0], inv_f, load_sem.at[1])
    load_diag = pltpu.make_async_copy(diag_hbm.at[0], diag_f, load_sem.at[2])
    load_off = pltpu.make_async_copy(off_hbm.at[0], off_f, load_sem.at[3])
    load_rd = pltpu.make_async_copy(rd_hbm.at[0], rd_v, load_sem.at[4])
    load_ro = pltpu.make_async_copy(ro_hbm.at[0], ro_v, load_sem.at[5])
    load_pat = pltpu.make_async_copy(pat_hbm.at[0], pat_ref, load_sem.at[6])
    own = pltpu.make_async_copy(vals_hbm.at[:, f, r, :], recv.at[f, r], own_sem)
    for load in (load_rows, load_inv, load_diag, load_off, load_rd, load_ro, load_pat, own):
        load.start()

    def exchange(pf, pr, source):
        return pltpu.make_async_remote_copy(
            src_ref=vals_hbm.at[:, pf, pr, :],
            dst_ref=recv.at[source // nr, lax.rem(source, nr)],
            send_sem=a2a_send.at[pf * nr + pr],
            recv_sem=a2a_recv.at[source],
            device_id=(pf, pr),
            device_id_type=MESH,
        )

    def source_of(s):
        i = lax.rem(s, members)
        return i // per, (s // members) * per + lax.rem(i, per)

    def prepare():
        load_rows.wait()

        def mark(s, c):
            sf, sr = source_of(s)
            code = rows_v[pl.ds(sf * nr + sr, 1), :] + (PART - rd)
            code_ref[pl.ds(s, 1), :] = code
            ids = lax.broadcasted_iota(jnp.int32, (PART, slot), 0)
            at = pl.ds(pl.multiple_of(s * slot, slot), slot)
            hot[:, at] = jnp.where((code & (PART - 1)) == ids, 1.0, 0.0).astype(jnp.bfloat16)
            return c

        lax.fori_loop(0, devices, mark, 0)

        load_inv.wait()
        for p in range(panels):
            def split_inv(i, c, p=p):
                at = pl.ds(pl.multiple_of(i * 64, 64), 64)
                hi, lo = split(inv_f[p, at, :])
                inv_h[p, at, :] = hi
                inv_l[p, at, :] = lo
                return c

            lax.fori_loop(0, W // 64, split_inv, 0)
        load_diag.wait()

        def split_diag(i, c):
            at = pl.ds(pl.multiple_of(i * 16, 16), 16)
            hi, lo = split(diag_f[at, :])
            diag_h[at, :] = hi
            diag_l[at, :] = lo
            return c

        lax.fori_loop(0, rd // 16, split_diag, 0)

        for p in range(panels - 1):
            @pl.when(plane > p)
            def _(p=p):
                for n in range(2):
                    columns = pl.ds(n * (W // 2), W // 2)
                    left_h = diag_h[:, pl.ds(p * W, W)]
                    left_l = diag_l[:, pl.ds(p * W, W)]
                    right_h = inv_h[p, :, columns]
                    product = (jnp.dot(left_h, right_h, preferred_element_type=jnp.float32)
                               + jnp.dot(left_l, right_h, preferred_element_type=jnp.float32)
                               + jnp.dot(left_h, inv_l[p, :, columns], preferred_element_type=jnp.float32))
                    hi, lo = split(product)
                    step_h[p, :, columns] = hi
                    step_l[p, :, columns] = lo

    def split_lower():
        load_off.wait()

        def split_off(i, c):
            at = pl.ds(pl.multiple_of(i * 16, 16), 16)
            hi, lo = split(off_f[at, :])
            off_h[at, :] = hi
            off_l[at, :] = lo
            return c

        lax.fori_loop(0, od // 16, split_off, 0)

    early = plane < panels // 2
    pl.when(early)(prepare)
    pl.semaphore_wait(barrier, devices - 1)

    def target(t):
        i = lax.rem(t, members)
        pf = lax.rem(f + i // per, nf)
        pr = (t // members) * per + lax.rem(place + i, per)
        return pf, pr

    def send(t, c):
        pf, pr = target(t)

        @pl.when(pf * nr + pr != me)
        def _():
            exchange(pf, pr, me).start()

        return c

    lax.fori_loop(0, devices, send, 0)

    pl.when(jnp.logical_not(early))(prepare)
    pl.when(plane > 0)(split_lower)

    group = 4
    span = group * slot
    per_plane = members // group
    chunk = 2 * BR
    chunks = od // chunk
    lower_parts = list(range(1, chunks + 1))

    def columns_of(g):
        return pl.ds(pl.multiple_of(g * span, span), span)

    def picked(g, parts):
        block = code_ref[pl.ds(pl.multiple_of(g * group, group), group), :]
        part = jnp.concatenate([block[u:u + 1, :] for u in range(group)], axis=1) >> 8
        values = vs[:, columns_of(g)]
        rows = []
        for h in parts:
            mask = jnp.where(jnp.broadcast_to(part, (16, span)) == h, 1.0, 0.0).astype(jnp.bfloat16)
            rows.append(values * jnp.concatenate([mask] * (2 * nrhs // 16), axis=0))
        return jnp.concatenate(rows, axis=0)

    def take(g):
        for u in range(group):
            s = g * group + u
            sf, sr = source_of(s)

            @pl.when(sf * nr + sr != me)
            def _(sf=sf, sr=sr):
                exchange(sf, sr, sf * nr + sr).wait_recv()

            hi, lo = split(recv[sf, sr])
            at = pl.ds(pl.multiple_of(s * slot, slot), slot)
            vs[pl.ds(0, nrhs), at] = hi
            vs[pl.ds(nrhs, nrhs), at] = lo

    upper_rows = pl.ds(0, 2 * nrhs)
    lower_rows = pl.ds(2 * nrhs, 2 * nrhs * chunks)

    def add_all(g):
        acc[...] += dot_nt(picked(g, [0] + lower_parts), hot[:, columns_of(g)])

    def add_upper(g):
        acc[upper_rows, :] += dot_nt(picked(g, [0]), hot[:, columns_of(g)])

    def add_lower(g):
        acc[lower_rows, :] += dot_nt(picked(g, lower_parts), hot[:, columns_of(g)])

    def reduced(h):
        at = 2 * h * nrhs
        return acc[at:at + nrhs, :] + acc[at + nrhs:at + 2 * nrhs, :]

    acc[...] = jnp.zeros_like(acc)
    load_rd.wait()
    load_ro.wait()
    load_pat.wait()
    own.wait()
    order = reach(panels, plane)
    for q in order[:-1]:
        def near(i, c, q=q):
            g = q * per_plane + i
            take(g)
            add_all(g)
            return c

        lax.fori_loop(0, per_plane, near, 0)

    def far(i, c):
        g = order[-1] * per_plane + i
        take(g)
        add_upper(g)
        return c

    lax.fori_loop(0, per_plane, far, 0)
    upper[...] = rd_v[...] + reduced(0)[:, PART - rd:]

    def scatter_lower():
        def step(i, c):
            add_lower(order[-1] * per_plane + i)
            return c

        lax.fori_loop(0, per_plane, step, 0)
        for h in range(chunks):
            at = pl.ds(h * chunk, chunk)
            rem_ref[0, :, at] = ro_v[:, at] + reduced(h + 1)

    def off_update(p, piece2):
        def step(i, c):
            at = pl.ds(pl.multiple_of(i * chunk, chunk), chunk)
            columns = pl.ds(p * W, W)
            term = dot3(piece2, off_h[at, columns], off_l[at, columns])
            scaled = jnp.concatenate(
                [term[:, b * BR:(b + 1) * BR] * pat_ref[p, 2 * i + b].astype(jnp.float32) for b in range(2)], axis=1)
            rem_ref[0, :, at] -= scaled
            return c

        lax.fori_loop(0, chunks, step, 0)

    some = nrhs // CUTS

    def share(to, j, c):
        at = pl.ds(c * some, some)
        return pltpu.make_async_remote_copy(
            src_ref=rhsbuf.at[j, at, :],
            dst_ref=rhsbuf.at[j, at, :],
            send_sem=pan_send.at[to * CUTS + c],
            recv_sem=pan_recv.at[j * CUTS + c],
            device_id=(f, to),
            device_id_type=MESH,
        )

    def first_targets(p):
        if p == panels - 1:
            return [q * per + i for q in range(panels - 1) for i in range(per)]
        return [(p + 1) * per + lax.rem(place + i, per) for i in range(per)]

    def later_targets(p):
        targets = [p * per + lax.rem(place + i, per) for i in range(1, per)]
        if p < panels - 1:
            targets += [q * per + lax.rem(place + i, per)
                        for q in [*range(p + 2, panels), *range(p - 1, -1, -1)] for i in range(per)]
        return targets

    def offer(p, c):
        at = pl.ds(c * some, some)
        rhsbuf[r, at, :] = upper[at, :]
        for to in first_targets(p):
            share(to, r, c).start()

    def offer_rest(p):
        for to in later_targets(p):
            for c in range(CUTS):
                share(to, r, c).start()

    def finish(p, b2):
        piece = dot3(b2, inv_h[p], inv_l[p])
        for i in range(per):
            @pl.when(r == p * per + i)
            def _(i=i):
                solved_ref[0] = piece[:, i * rd:(i + 1) * rd]
        off_update(p, jnp.concatenate(split(piece), axis=0))

    @pl.when(plane == 0)
    def _():
        for c in range(CUTS):
            offer(0, c)
        offer_rest(0)

    b2 = None
    for p in range(panels):
        if p == 0:
            pl.when(plane == 0)(split_lower)
            scatter_lower()
        else:
            finish(p - 1, b2)

        owners = range(p * per, (p + 1) * per)
        for c in range(CUTS):
            at = pl.ds(c * some, some)
            for j in owners:
                @pl.when(r != j)
                def _(j=j, c=c):
                    share(j, j, c).wait_recv()

            if p < panels - 1:
                @pl.when(plane > p)
                def _(p=p, at=at):
                    part = jnp.concatenate([rhsbuf[j, at, :] for j in owners], axis=1)
                    upper[at, :] -= dot3(jnp.concatenate(split(part), axis=0), step_h[p], step_l[p])

                @pl.when(plane == p + 1)
                def _(p=p, c=c):
                    offer(p + 1, c)

        if p < panels - 1:
            @pl.when(plane == p + 1)
            def _(p=p):
                offer_rest(p + 1)

        b2 = jnp.concatenate(split(jnp.concatenate([rhsbuf[j] for j in owners], axis=1)), axis=0)

    finish(panels - 1, b2)

    def sent(t, c):
        pf, pr = target(t)

        @pl.when(pf * nr + pr != me)
        def _():
            exchange(pf, pr, me).wait_send()

        return c

    lax.fori_loop(0, devices, sent, 0)

    def shared(d, c):
        for c in range(CUTS):
            share(lax.rem(r + d, nr), r, c).wait_send()
        return c

    lax.fori_loop(1, nr, shared, 0)


def hand_out(solved_in, rem_in, solved_out, rem_out):
    solved_out[...] = solved_in[...]
    rem_out[...] = rem_in[...]


def local(nf, nr, rhs_diag, rhs_off, diag_factor, off_factor, diag_inverse, pattern, upd_vals, upd_rows):
    nrhs = upd_vals.shape[0]
    slot = upd_vals.shape[5]
    rd = diag_factor.shape[1]
    od = off_factor.shape[1]
    k = diag_factor.shape[2]
    panels = diag_inverse.shape[1]
    devices = nf * nr
    parts = od // PART + 1
    vals = upd_vals.reshape(upd_vals.shape[0], nf, nr, slot)
    rows = upd_rows.reshape(devices, slot)
    vmem = pl.BlockSpec(memory_space=pltpu.VMEM)
    anywhere = pl.BlockSpec(memory_space=pl.ANY)
    f32, bf16 = jnp.float32, jnp.bfloat16
    outs = (
        jax.ShapeDtypeStruct((1, nrhs, rd), f32),
        jax.ShapeDtypeStruct((1, nrhs, od), f32),
    )
    results = pl.pallas_call(
        functools.partial(kernel, nf, nr),
        out_shape=(pltpu.VMEM((1, nrhs, rd), f32), pltpu.VMEM((1, nrhs, od), f32)),
        in_specs=[anywhere] * 8,
        out_specs=(vmem, vmem),
        scratch_shapes=[
            pltpu.VMEM((rd, k), f32),
            pltpu.VMEM((od, k), f32),
            pltpu.VMEM((panels, W, W), f32),
            pltpu.VMEM((rd, k), bf16),
            pltpu.VMEM((rd, k), bf16),
            pltpu.VMEM((od, k), bf16),
            pltpu.VMEM((od, k), bf16),
            pltpu.VMEM((panels, W, W), bf16),
            pltpu.VMEM((panels, W, W), bf16),
            pltpu.VMEM((panels - 1, rd, W), bf16),
            pltpu.VMEM((panels - 1, rd, W), bf16),
            pltpu.VMEM((nf, nr, nrhs, slot), f32),
            pltpu.VMEM((2 * nrhs, devices * slot), bf16),
            pltpu.VMEM((PART, devices * slot), bf16),
            pltpu.VMEM((devices, slot), jnp.int32),
            pltpu.VMEM((devices, slot), jnp.int32),
            pltpu.VMEM((2 * nrhs * parts, PART), f32),
            pltpu.VMEM((nrhs, rd), f32),
            pltpu.VMEM((nr, nrhs, rd), f32),
            pltpu.VMEM((nrhs, rd), f32),
            pltpu.VMEM((nrhs, od), f32),
            pltpu.SMEM(pattern.shape[1:], jnp.int32),
            pltpu.SemaphoreType.DMA((7,)),
            pltpu.SemaphoreType.DMA,
            pltpu.SemaphoreType.DMA((devices,)),
            pltpu.SemaphoreType.DMA((devices,)),
            pltpu.SemaphoreType.DMA((nr * CUTS,)),
            pltpu.SemaphoreType.DMA((nr * CUTS,)),
        ],
        compiler_params=pltpu.CompilerParams(
            collective_id=0, has_side_effects=True, vmem_limit_bytes=58 * 1024 * 1024),
    )(rhs_diag, rhs_off, diag_factor, off_factor, diag_inverse, pattern, vals, rows)
    return pl.pallas_call(hand_out, out_shape=outs, in_specs=[vmem, vmem], out_specs=(vmem, vmem),
        compiler_params=pltpu.CompilerParams(vmem_limit_bytes=1024 * 1024))(*results)


def solution(mesh):
    in_specs = (
        P("front", None, "row"),
        P("front", None, "row"),
        P("front", "row", None),
        P("front", "row", None),
        P("front", None, None, None),
        P("front", None, "row"),
        P(None, "front", "row", None, None, None),
        P("front", "row", None, None, None),
    )
    out_specs = (P("front", None, "row"), P("front", None, "row"))
    body = functools.partial(local, mesh.shape["front"], mesh.shape["row"])
    return jax.shard_map(body, mesh=mesh, in_specs=in_specs, out_specs=out_specs, check_vma=False)
```
